512 devices in a mesh: tm: 32 (over y, x), pts: 16 (over z, core).
Axes of the slice: x: 4, y: 8, z: 8, core: 2. Of those that a mesh axis runs over, the one named last changes fastest.
Arguments:
- snapshots: bfloat16 [16, 512, 5, 4096], P(None, 'tm', None, 'pts'), may hold values from -8 to 8
- weights: float32 [5, 4096], P(None, 'pts'), may hold values from 1.953125e-05 to 0.0001953125
- freq_bins: int32 [256], replicated, may hold values from 0 to 255, as said below
- bin_owners: int32 [256], replicated, may hold values from 0 to 31, as said below
Outputs:
- csd: float32 [512, 512], P('tm')
The draws below stay inside these ranges and needn't reach their ends.
Inputs may be any that keep to these rules, and one draw needn't show every extreme that they name: `freq_bins`: the listed bins are distinct. `bin_owners`: no owner holds more than 16 listed bins and one holds exactly 16; owners hold uneven numbers of bins.
All inputs are finite; a program needn't handle non-finite values.
Results may differ from the reference program's by a relative error of at most 0.00053.
Values may be sent and summed in bfloat16 or wider, within the bound.
No kernel may reach another device: no remote copies, remote signals or barrier semaphores. Data moves between devices by JAX's collectives and lax.ppermute only.
A program may use at most 64 MiB of HBM per device.

```python
import math
import jax
import jax.numpy as jnp
from jax import lax

NB = 16
NFFT = 512
NF = 5
CAP = 16
NK = 256
NP = 4096
N_TM = 32


def draw_snapshots(key, part):
    key_noise, key_common = jax.random.split(jax.random.fold_in(key, 11), 2)
    common = jax.random.normal(key_common, (1, NFFT, NF, NP), jnp.float32)
    noise = jax.random.normal(key_noise, (NB, NFFT, NF, NP), jnp.float32)
    values = noise + 0.8 * common
    return jnp.clip(values, -8.0, 8.0).astype(jnp.bfloat16)


def draw_freq_bins(key, part):
    order = jax.random.permutation(jax.random.fold_in(key, 23), NFFT // 2)
    return order[:NK].astype(jnp.int32)


def draw_bin_owners(key, part):
    key_order, key_share, key_shuffle = jax.random.split(jax.random.fold_in(key, 37), 3)
    half = N_TM // 2
    order = jax.random.permutation(key_order, N_TM).astype(jnp.int32)
    share = jax.random.randint(key_share, (half,), 0, CAP + 1).astype(jnp.int32)
    share = share.at[0].set(CAP)
    counts = jnp.zeros((N_TM,), jnp.int32).at[order[:half]].set(share).at[order[half:]].set(CAP - share)
    ends = jnp.cumsum(counts)
    sorted_owner = jnp.sum((jnp.arange(NK, dtype=jnp.int32)[:, None] >= ends[None, :]).astype(jnp.int32), axis=1)
    shuffle = jax.random.permutation(key_shuffle, NK)
    return sorted_owner[shuffle].astype(jnp.int32)


def block_levels(rng, dims, cuts, low, top_value):
    level = 1.0
    for axis_at, parts in cuts:
        steps = jax.random.uniform(jax.random.fold_in(jax.random.fold_in(rng, 6), axis_at), (parts,), jnp.float32, low / len(cuts), top_value / len(cuts))
        level = level * jnp.repeat(jnp.exp(steps), dims[axis_at] // parts).reshape((-1,) + (1,) * (len(dims) - 1 - axis_at))
    return level


def setup_inputs(seed: int = 0) -> dict:
    arg_keys = jax.random.split(jax.random.key(seed), 5)
    return {
        "snapshots": draw_snapshots(jax.random.fold_in(arg_keys[4], 71), 0),
        "weights": jnp.clip(jnp.exp(math.log(0.0001953125) - 2.3025851 * jax.random.uniform(arg_keys[1], (NF, NP), jnp.float32) ** block_levels(arg_keys[1], (NF, NP), ((1, 16),), -0.2, 0.2)), 1.9531249563442543e-05, 0.0001953125),
        "freq_bins": draw_freq_bins(jax.random.fold_in(arg_keys[4], 71), 0),
        "bin_owners": draw_bin_owners(jax.random.fold_in(arg_keys[4], 71), 0),
    }


def slot_index(bin_owners, owner_count):
    owner_ids = jnp.arange(owner_count, dtype=jnp.int32)
    onehot = (bin_owners[:, None] == owner_ids[None, :]).astype(jnp.int32)
    before = jnp.cumsum(onehot, axis=0) - onehot
    position = lax.optimization_barrier(jnp.sum(before * onehot, axis=1))
    return (bin_owners * CAP + position).astype(jnp.int32)

def dft_rows(bin_values, live_mask, fft_len):
    steps_t = jnp.arange(fft_len, dtype=jnp.int32)
    wound = bin_values[:, None] * steps_t[None, :] % fft_len
    angles = 2.0 * jnp.pi * wound.astype(jnp.float32) / fft_len
    hann_window = 0.5 - 0.5 * jnp.cos(2.0 * jnp.pi * steps_t.astype(jnp.float32) / fft_len)
    scaled = hann_window / jnp.sqrt(jnp.float32(3.0 * fft_len / 8.0))
    scaled = scaled[None, :] * live_mask[:, None]
    cosine = (scaled * jnp.cos(angles)).astype(jnp.bfloat16)
    sine_rows = (-scaled * jnp.sin(angles)).astype(jnp.bfloat16)
    return jnp.stack([cosine, sine_rows], axis=1).reshape(-1, fft_len)

def fold_gram(gram_mat, blocks):
    real_part = gram_mat[..., :blocks, :blocks] + gram_mat[..., blocks:, blocks:]
    imag_part = gram_mat[..., :blocks, blocks:] - gram_mat[..., blocks:, :blocks]
    leading = gram_mat.shape[:-2]
    return jnp.concatenate([real_part.reshape(leading + (blocks * blocks,)), imag_part.reshape(leading + (blocks * blocks,))], axis=-1)

def reference(snapshots, weights, freq_bins, bin_owners):
    blocks, fft_len, fields, points = snapshots.shape
    columns = fields * points
    by_time = jnp.transpose(snapshots.reshape(blocks, fft_len, columns), (1, 0, 2)).reshape(fft_len, blocks * columns)
    weight_row = weights.reshape(columns)

    def one_group(group_bins):
        dft_table = dft_rows(group_bins, jnp.ones(group_bins.shape, jnp.float32), fft_len)
        spectra = jnp.dot(dft_table, by_time, preferred_element_type=jnp.float32).astype(jnp.bfloat16)
        spectra = spectra.reshape(-1, 2 * blocks, columns)
        weighted = (spectra.astype(jnp.float32) * weight_row).astype(jnp.bfloat16)
        gram_mat = jnp.einsum('gac,gbc->gab', spectra.astype(jnp.float32), weighted.astype(jnp.float32), precision=lax.Precision.HIGHEST)
        return fold_gram(gram_mat, blocks)
    group_csd = lax.map(one_group, freq_bins.reshape(-1, 8))
    bin_csd = group_csd.reshape(-1, 2 * blocks * blocks)
    slot_ids = slot_index(bin_owners, N_TM)
    result = jnp.zeros((N_TM * CAP, 2 * blocks * blocks), jnp.float32)
    return result.at[slot_ids].set(bin_csd)
```

```python
import functools

import jax
import jax.numpy as jnp
import numpy as np
from jax import lax
from jax.experimental import pallas as pl
from jax.experimental.pallas import tpu as pltpu
from jax.sharding import PartitionSpec as P

CAP = 16
LANES = 128


def dft_rows(bin_values, fft_len):
    steps_t = jnp.arange(fft_len, dtype=jnp.int32)
    wound = bin_values[:, None] * steps_t[None, :] % fft_len
    angles = 2.0 * jnp.pi * wound.astype(jnp.float32) / fft_len
    hann_window = 0.5 - 0.5 * jnp.cos(2.0 * jnp.pi * steps_t.astype(jnp.float32) / fft_len)
    scaled = hann_window / jnp.sqrt(jnp.float32(3.0 * fft_len / 8.0))
    cosine = (scaled * jnp.cos(angles)).astype(jnp.bfloat16)
    sine_rows = (-scaled * jnp.sin(angles)).astype(jnp.bfloat16)
    return jnp.concatenate([cosine, sine_rows], axis=0)


def slot_rows(bin_owners, slot_count):
    count = bin_owners.shape[0]
    listed = jnp.arange(count, dtype=jnp.int32)
    same = (bin_owners[:, None] == bin_owners[None, :]) & (listed[None, :] < listed[:, None])
    position = jnp.sum(same.astype(jnp.int32), axis=1)
    slots = bin_owners * CAP + position
    return (jnp.arange(slot_count, dtype=jnp.int32)[:, None] == slots[None, :]).astype(jnp.bfloat16)


def scatter_body(x_ref, out_ref):
    blocks, fields = x_ref.shape[0], x_ref.shape[1]
    group = lax.broadcasted_iota(jnp.int32, x_ref.shape[2:], 1) // (LANES // blocks)
    width = LANES // blocks
    for f in range(fields):
        rows = []
        for b in range(blocks):
            row = x_ref[b, f].astype(jnp.float32)
            rows.append(pltpu.roll(row, width * b, 1) if b else row)
        bit = 1
        while bit < blocks:
            take = (group & bit) != 0
            rows = [jnp.where(take, rows[(c + bit) % blocks], rows[c]) for c in range(blocks)]
            bit *= 2
        for d in range(blocks):
            row = rows[(blocks - d) % blocks]
            if d:
                row = pltpu.roll(row, LANES - width * d, 1)
            out_ref[d, f] = row.astype(jnp.bfloat16)


def scatter_points(x):
    blocks, fields, steps, points = x.shape
    tiles = points // LANES
    return pl.pallas_call(
        scatter_body,
        grid=(tiles,),
        out_shape=jax.ShapeDtypeStruct((blocks * tiles, fields, steps, LANES), jnp.bfloat16),
        in_specs=[pl.BlockSpec((blocks, fields, steps, LANES), lambda h: (0, 0, 0, h))],
        out_specs=pl.BlockSpec((blocks, fields, steps, LANES), lambda h: (h, 0, 0, 0)),
        name="scatter_points",
    )(x)


def split2(value):
    high = value.astype(jnp.bfloat16)
    return high, (value - high.astype(jnp.float32)).astype(jnp.bfloat16)


def gram_body(x_ref, table_ref, w_ref, pick_ref, slot_ref, out_ref, spec, high, low):
    fields = x_ref.shape[1]
    steps = x_ref.shape[0] * x_ref.shape[2]
    count = table_ref.shape[0] // 2
    for f in range(fields):
        part = jnp.dot(
            table_ref[...],
            x_ref[:, f].reshape(steps, LANES),
            preferred_element_type=jnp.float32,
        )
        spec[f] = part.astype(jnp.bfloat16).astype(jnp.float32)
    rows = 16
    left = lax.broadcasted_iota(jnp.int32, (rows, LANES), 1) < LANES // 2

    def chunk(c, carry):
        at = pl.multiple_of(c * rows, rows)
        re = [spec[f, pl.ds(at, rows), :] for f in range(fields)]
        im = [spec[f, pl.ds(count + at, rows), :] for f in range(fields)]
        wre = [re[f] * w_ref[f : f + 1, :] for f in range(fields)]
        wim = [im[f] * w_ref[f : f + 1, :] for f in range(fields)]

        def put(j, value):
            hi, lo = split2(value)
            high[pl.ds(at, rows), j * LANES : (j + 1) * LANES] = hi
            low[pl.ds(at, rows), j * LANES : (j + 1) * LANES] = lo

        for delta in range(9):
            if delta:
                qre = [pltpu.roll(v, LANES - 8 * delta, 1) for v in wre]
                qim = [pltpu.roll(v, LANES - 8 * delta, 1) for v in wim]
            else:
                qre, qim = wre, wim
            real = sum(re[f] * qre[f] + im[f] * qim[f] for f in range(fields))
            if delta == 0:
                put(0, real)
                continue
            imag = sum(re[f] * qim[f] - im[f] * qre[f] for f in range(fields))
            if delta < 8:
                put(delta, real)
                put(delta + 7, imag)
            else:
                put(15, jnp.where(left, real, pltpu.roll(imag, LANES // 2, 1)))
        return carry

    lax.fori_loop(0, count // rows, chunk, 0)
    packed = jnp.dot(high[...], pick_ref[...], preferred_element_type=jnp.float32) + jnp.dot(
        low[...], pick_ref[...], preferred_element_type=jnp.float32
    )
    hi, lo = split2(packed)
    out_ref[...] = jnp.dot(slot_ref[...], hi, preferred_element_type=jnp.float32) + jnp.dot(
        slot_ref[...], lo, preferred_element_type=jnp.float32
    )


def gram_sums(by_point, table, lane_weights, pick, slots):
    fields = by_point.shape[1]
    count = table.shape[0] // 2
    wide = 16 * LANES
    return pl.pallas_call(
        gram_body,
        out_shape=jax.ShapeDtypeStruct((slots.shape[0], 256), jnp.float32),
        scratch_shapes=[
            pltpu.VMEM((fields, 2 * count, LANES), jnp.float32),
            pltpu.VMEM((count, wide), jnp.bfloat16),
            pltpu.VMEM((count, wide), jnp.bfloat16),
        ],
        name="gram_sums",
    )(by_point, table, lane_weights, pick, slots)


def unpack_matrix(blocks):
    table = np.zeros((256, 2 * blocks * blocks), np.float32)
    half = blocks // 2
    for b in range(blocks):
        for e in range(blocks):
            delta = (e - b) % blocks
            if delta < half:
                real, imag, sign = 16 * delta + b, 16 * (delta + 7) + b, 1.0
            elif delta == half:
                real, imag, sign = 240 + b % half, 248 + b % half, 1.0 if b < half else -1.0
            else:
                back = blocks - delta
                real, imag, sign = 16 * back + e, 16 * (back + 7) + e, -1.0
            table[real, b * blocks + e] = 1.0
            if delta:
                table[imag, blocks * blocks + b * blocks + e] = sign
    return table


def shards(snapshots, weights, freq_bins, bin_owners):
    blocks, local_steps, fields, points = snapshots.shape
    tm_count = lax.axis_size("tm")
    pts_count = lax.axis_size("pts")
    fft_len = local_steps * tm_count
    sub_points = points // tm_count
    slot_count = tm_count * CAP
    sent = scatter_points(jnp.transpose(snapshots, (0, 2, 1, 3)))
    by_point = lax.all_to_all(sent, "tm", split_axis=0, concat_axis=0, tiled=True)
    table = dft_rows(freq_bins, fft_len)
    slots = slot_rows(bin_owners, slot_count)
    mine = lax.dynamic_slice(weights, (0, lax.axis_index("tm") * sub_points), (fields, sub_points))
    lane_weights = jnp.tile(mine, (1, blocks))
    pick = (
        jnp.arange(16 * LANES, dtype=jnp.int32)[:, None] // 8
        == jnp.arange(256, dtype=jnp.int32)[None, :]
    ).astype(jnp.bfloat16)
    partial = gram_sums(by_point, table, lane_weights, pick, slots)
    partial = partial.reshape(tm_count, CAP, 256)
    owned = jnp.sum(lax.all_to_all(partial, "tm", split_axis=0, concat_axis=0, tiled=True), axis=0)
    row = jnp.sum(lax.all_to_all(owned, "pts", split_axis=0, concat_axis=0, tiled=True), axis=0)
    rows = jnp.broadcast_to(row[None, :], (pts_count, 256))
    summed = lax.all_to_all(rows, "pts", split_axis=0, concat_axis=0, tiled=True)
    return jnp.dot(
        summed, jnp.asarray(unpack_matrix(blocks)), precision=lax.Precision.HIGHEST
    )


def solution(mesh):
    in_specs = (P(None, "tm", None, "pts"), P(None, "pts"), P(), P())
    out_specs = P("tm", None)
    return jax.shard_map(shards, mesh=mesh, in_specs=in_specs, out_specs=out_specs, check_vma=False)
```

```python
import functools

import jax
import jax.numpy as jnp
import numpy as np
from jax import lax
from jax.experimental import pallas as pl
from jax.experimental.pallas import tpu as pltpu
from jax.sharding import PartitionSpec as P

CAP = 16
LANES = 128


def dft_columns(bin_values, fft_len):
    steps_t = jnp.arange(fft_len, dtype=jnp.int32)[:, None]
    wound = bin_values[None, :] * steps_t % fft_len
    angles = 2.0 * jnp.pi * wound.astype(jnp.float32) / fft_len
    hann_window = 0.5 - 0.5 * jnp.cos(2.0 * jnp.pi * steps_t.astype(jnp.float32) / fft_len)
    scaled = hann_window / jnp.sqrt(jnp.float32(3.0 * fft_len / 8.0))
    cosine = (scaled * jnp.cos(angles)).astype(jnp.bfloat16)
    sine_rows = (-scaled * jnp.sin(angles)).astype(jnp.bfloat16)
    return jnp.concatenate([cosine, sine_rows], axis=1)


def slot_rows(bin_owners, slot_count):
    count = bin_owners.shape[0]
    listed = jnp.arange(count, dtype=jnp.int32)
    same = (bin_owners[:, None] == bin_owners[None, :]) & (listed[None, :] < listed[:, None])
    position = jnp.sum(same.astype(jnp.int32), axis=1)
    slots = bin_owners * CAP + position
    return (jnp.arange(slot_count, dtype=jnp.int32)[:, None] == slots[None, :]).astype(jnp.bfloat16)


def scatter_body(x_ref, out_ref):
    blocks, fields, steps = x_ref.shape[:3]
    groups = 16
    width = LANES // groups
    group = lax.broadcasted_iota(jnp.int32, (steps, LANES), 1) // width
    sources = []
    for pair in range(fields // 2):
        for first in range(0, blocks, groups // 2):
            sources.append([(first + g // 2, 2 * pair + g % 2) for g in range(groups)])
    sources.append([(g, fields - 1) for g in range(groups)])
    for tile, source in enumerate(sources):
        rows = []
        for g, (b, f) in enumerate(source):
            row = x_ref[b, f].astype(jnp.float32)
            rows.append(pltpu.roll(row, width * g, 1) if g else row)
        bit = 1
        while bit < groups:
            take = (group & bit) != 0
            rows = [jnp.where(take, rows[(c + bit) % groups], rows[c]) for c in range(groups)]
            bit *= 2
        for d in range(groups):
            row = rows[(groups - d) % groups]
            if d:
                row = pltpu.roll(row, LANES - width * d, 1)
            out_ref[d, :, tile * LANES : (tile + 1) * LANES] = row.astype(jnp.bfloat16)


def scatter_points(x):
    blocks, fields, steps, points = x.shape
    tiles = points // LANES
    wide = fields * blocks * points // (16 * tiles)
    return pl.pallas_call(
        scatter_body,
        grid=(tiles,),
        out_shape=jax.ShapeDtypeStruct((16 * tiles, steps, wide), jnp.bfloat16),
        in_specs=[pl.BlockSpec((blocks, fields, steps, LANES), lambda h: (0, 0, 0, h))],
        out_specs=pl.BlockSpec((16, steps, wide), lambda h: (h, 0, 0)),
        name="scatter_points",
    )(x)


def gram_body(x_ref, table_ref, w_ref, slot_ref, out_ref, plain, weighted, sums, packed):
    steps = x_ref.shape[0] * x_ref.shape[1]
    count = table_ref.shape[1] // 2
    wide = x_ref.shape[2]
    tiles = wide // LANES
    for tile in range(tiles):
        cols = slice(tile * LANES, (tile + 1) * LANES)
        spec = lax.dot_general(
            x_ref[:, :, cols].reshape(steps, LANES),
            table_ref[...],
            (((0,), (0,)), ((), ())),
            preferred_element_type=jnp.float32,
        )
        spec = spec.astype(jnp.bfloat16).astype(jnp.float32)
        row_w = w_ref[cols, :]
        scaled = spec * jnp.concatenate([row_w] * (2 * count // LANES), axis=1)
        if tile < tiles - 1:
            half, at = tile // 2, tile % 2 * LANES
            plain[half, at : at + LANES, :] = spec.astype(jnp.bfloat16)
            scaled = scaled.astype(jnp.bfloat16)
            weighted[half, at : at + LANES, :] = scaled
            if at == 0:
                weighted[half, 2 * LANES :, :] = scaled
        else:
            half = tiles // 2
            gap = jnp.zeros((16, 8, 2 * count), jnp.float32)
            for ref, value in ((plain, spec), (weighted, scaled)):
                value = jnp.concatenate([value.reshape(16, 8, 2 * count), gap], axis=1)
                value = value.reshape(2 * LANES, 2 * count).astype(jnp.bfloat16)
                ref[half, : 2 * LANES, :] = value
                if ref is weighted:
                    ref[half, 2 * LANES :, :] = value[:LANES]
    halves = plain.shape[0]

    def block(b, last):
        at = pl.multiple_of(b * 16, 16)
        re = [plain[h, pl.ds(at, 16), :count] for h in range(halves)]
        im = [plain[h, pl.ds(at, 16), count:] for h in range(halves)]
        for delta in range(last + 1):
            to = pl.multiple_of(at + delta * 16, 16)
            qre = [weighted[h, pl.ds(to, 16), :count] for h in range(halves)]
            qim = [weighted[h, pl.ds(to, 16), count:] for h in range(halves)]
            real = sum(re[h] * qre[h] + im[h] * qim[h] for h in range(halves))
            where = delta if delta < 8 else 15
            sums[pl.ds(pl.multiple_of(where * 256 + at, 16), 16), :] = real
            if delta:
                imag = sum(re[h] * qim[h] - im[h] * qre[h] for h in range(halves))
                offset = (delta + 7) * 256 if delta < 8 else 15 * 256 + 128
                sums[pl.ds(pl.multiple_of(offset + at, 16), 16), :] = imag

    lax.fori_loop(0, 8, lambda b, carry: (block(b, 8), carry)[1], 0)
    lax.fori_loop(8, 16, lambda b, carry: (block(b, 7), carry)[1], 0)
    sel = lax.broadcasted_iota(jnp.int32, (16, 256), 1) // 16
    sel = (sel == lax.broadcasted_iota(jnp.int32, (16, 256), 0)).astype(jnp.bfloat16)
    for j in range(16):
        part = jnp.dot(sel, sums[j * 256 : (j + 1) * 256, :], preferred_element_type=jnp.float32)
        packed[j * 16 : (j + 1) * 16, :] = part.astype(jnp.bfloat16)
    out_ref[...] = lax.dot_general(
        slot_ref[...],
        packed[...],
        (((1,), (1,)), ((), ())),
        preferred_element_type=jnp.float32,
    ).astype(jnp.bfloat16)


def gram_sums(by_point, table, row_weights, slots):
    count = table.shape[1] // 2
    halves = (by_point.shape[2] // LANES + 1) // 2
    vmem = pl.BlockSpec(memory_space=pltpu.VMEM)
    return pl.pallas_call(
        gram_body,
        out_shape=jax.ShapeDtypeStruct((slots.shape[0], 256), jnp.bfloat16),
        in_specs=[vmem] * 4,
        out_specs=vmem,
        scratch_shapes=[
            pltpu.VMEM((halves, 256, 2 * count), jnp.bfloat16),
            pltpu.VMEM((halves, 384, 2 * count), jnp.bfloat16),
            pltpu.VMEM((256 * 16, count), jnp.bfloat16),
            pltpu.VMEM((256, count), jnp.bfloat16),
        ],
        compiler_params=pltpu.CompilerParams(vmem_limit_bytes=24 * 1024 * 1024),
        name="gram_sums",
    )(by_point, table, row_weights, slots)


def unpack_matrix(blocks):
    table = np.zeros((256, 2 * blocks * blocks), np.float32)
    half = blocks // 2
    for b in range(blocks):
        for e in range(blocks):
            delta = (e - b) % blocks
            if delta < half:
                real, imag, sign = 16 * delta + b, 16 * (delta + 7) + b, 1.0
            elif delta == half:
                real, imag, sign = 240 + b % half, 248 + b % half, 1.0 if b < half else -1.0
            else:
                back = blocks - delta
                real, imag, sign = 16 * back + e, 16 * (back + 7) + e, -1.0
            table[real, b * blocks + e] = 1.0
            if delta:
                table[imag, blocks * blocks + b * blocks + e] = sign
    return table


def shards(snapshots, weights, freq_bins, bin_owners):
    blocks, local_steps, fields, points = snapshots.shape
    tm_count = lax.axis_size("tm")
    pts_count = lax.axis_size("pts")
    fft_len = local_steps * tm_count
    sub_points = points // tm_count
    slot_count = tm_count * CAP
    sent = scatter_points(jnp.transpose(snapshots, (0, 2, 1, 3)))
    by_point = lax.all_to_all(sent, "tm", split_axis=0, concat_axis=0, tiled=True)
    table = dft_columns(freq_bins, fft_len)
    slots = slot_rows(bin_owners, slot_count)
    mine = lax.dynamic_slice(weights, (0, lax.axis_index("tm") * sub_points), (fields, sub_points))
    paired = jnp.broadcast_to(
        mine[: fields - 1].reshape(fields // 2, 1, 2, sub_points),
        (fields // 2, blocks, 2, sub_points),
    )
    single = jnp.broadcast_to(mine[fields - 1 :], (blocks, sub_points))
    row_weights = jnp.concatenate([paired.reshape(-1), single.reshape(-1)])
    row_weights = jnp.broadcast_to(row_weights[:, None], (row_weights.shape[0], LANES))
    partial = gram_sums(by_point, table, row_weights, slots)
    partial = partial.reshape(tm_count, CAP, 256)
    partial = lax.all_to_all(partial, "tm", split_axis=0, concat_axis=0, tiled=True)
    owned = jnp.sum(partial.astype(jnp.float32), axis=0)
    copies = jnp.broadcast_to(owned[None], (pts_count,) + owned.shape)
    copies = lax.all_to_all(copies, "pts", split_axis=0, concat_axis=0, tiled=True)
    summed = jnp.sum(copies, axis=0)
    return jnp.dot(
        summed, jnp.asarray(unpack_matrix(blocks)), precision=lax.Precision.HIGHEST
    )


def solution(mesh):
    in_specs = (P(None, "tm", None, "pts"), P(None, "pts"), P(), P())
    out_specs = P("tm", None)
    return jax.shard_map(shards, mesh=mesh, in_specs=in_specs, out_specs=out_specs, check_vma=False)
```

```python
import functools

import jax
import jax.numpy as jnp
import numpy as np
from jax import lax
from jax.experimental import pallas as pl
from jax.experimental.pallas import tpu as pltpu
from jax.sharding import PartitionSpec as P

CAP = 16
LANES = 128


def dft_columns(bin_values, fft_len):
    steps_t = jnp.arange(fft_len, dtype=jnp.int32)[:, None]
    wound = bin_values[None, :] * steps_t % fft_len
    angles = 2.0 * jnp.pi * wound.astype(jnp.float32) / fft_len
    hann_window = 0.5 - 0.5 * jnp.cos(2.0 * jnp.pi * steps_t.astype(jnp.float32) / fft_len)
    scaled = hann_window / jnp.sqrt(jnp.float32(3.0 * fft_len / 8.0))
    cosine = (scaled * jnp.cos(angles)).astype(jnp.bfloat16)
    sine_rows = (-scaled * jnp.sin(angles)).astype(jnp.bfloat16)
    return jnp.concatenate([cosine, sine_rows], axis=1)


def slot_rows(bin_owners, owner_count, core):
    count = bin_owners.shape[0]
    listed = jnp.arange(count, dtype=jnp.int32)
    same = (bin_owners[:, None] == bin_owners[None, :]) & (listed[None, :] < listed[:, None])
    position = jnp.sum(same.astype(jnp.int32), axis=1)
    part = CAP // 2
    side = position // part
    row = (side != core).astype(jnp.int32) * (owner_count * part)
    row = row + bin_owners * part + position % part
    return (jnp.arange(owner_count * CAP, dtype=jnp.int32)[:, None] == row[None, :]).astype(
        jnp.bfloat16
    )


def lane_tiles(blocks, fields):
    tiles = []
    for pair in range(fields // 2):
        for first in range(0, blocks, 8):
            tiles.append([(first + g // 2, 2 * pair + g % 2) for g in range(16)])
    return tiles + [[(g, fields - 1) for g in range(16)]]


def scatter_body(x_ref, out_ref, held, ready, arrived, left):
    blocks, fields, steps, points = x_ref.shape
    groups = 16
    width = LANES // groups
    group = lax.broadcasted_iota(jnp.int32, (steps, LANES), 1) // width
    tiles = lane_tiles(blocks, fields)
    copies = []
    for tile, source in enumerate(tiles):
        firsts, lasts = source[0], source[-1]
        part = (slice(firsts[0], lasts[0] + 1), slice(firsts[1], lasts[1] + 1))
        copies.append(pltpu.make_async_copy(x_ref.at[part], held.at[part], arrived.at[tile]))
        copies[-1].start()
    for tile, source in enumerate(tiles):
        copies[tile].wait()
        for h in range(points // LANES):
            rows = []
            for g, (b, f) in enumerate(source):
                row = held[b, f, :, h * LANES : (h + 1) * LANES]
                rows.append(pltpu.roll(row, width * g, 1) if g else row)
            bit = 1
            while bit < groups:
                take = (group & bit) != 0
                rows = [jnp.where(take, rows[(c + bit) % groups], rows[c]) for c in range(groups)]
                bit *= 2
            for d in range(groups):
                row = rows[(groups - d) % groups]
                if d:
                    row = pltpu.roll(row, LANES - width * d, 1)
                ready[tile, h * groups + d] = row
        lanes = slice(tile * LANES, (tile + 1) * LANES)
        copies[tile] = pltpu.make_async_copy(ready.at[tile], out_ref.at[:, :, lanes], left.at[tile])
        copies[tile].start()
    for copy in copies:
        copy.wait()


def scatter_points(x):
    blocks, fields, steps, points = x.shape
    tiles = len(lane_tiles(blocks, fields))
    wide = tiles * LANES
    return pl.pallas_call(
        scatter_body,
        out_shape=jax.ShapeDtypeStruct((points // 8, steps, wide), jnp.bfloat16),
        in_specs=[pl.BlockSpec(memory_space=pltpu.HBM)],
        out_specs=pl.BlockSpec(memory_space=pltpu.HBM),
        scratch_shapes=[
            pltpu.VMEM(x.shape, jnp.bfloat16),
            pltpu.VMEM((tiles, points // 8, steps, LANES), jnp.bfloat16),
            pltpu.SemaphoreType.DMA((tiles,)),
            pltpu.SemaphoreType.DMA((tiles,)),
        ],
        name="scatter_points",
    )(x)


def split2(value):
    high = value.astype(jnp.bfloat16)
    return high, (value - high.astype(jnp.float32)).astype(jnp.bfloat16)


def gram_body(x_ref, table_ref, w_ref, slot_ref, keep_ref, send_ref, plain, weighted, sums, high, low):
    steps = x_ref.shape[0] * x_ref.shape[1]
    count = table_ref.shape[1] // 2
    tiles = x_ref.shape[2] // LANES
    for tile in range(tiles):
        cols = slice(tile * LANES, (tile + 1) * LANES)
        spec = lax.dot_general(
            x_ref[:, :, cols].reshape(steps, LANES),
            table_ref[...],
            (((0,), (0,)), ((), ())),
            preferred_element_type=jnp.float32,
        )
        spec = spec.astype(jnp.bfloat16).astype(jnp.float32)
        scaled = spec * jnp.concatenate([w_ref[cols, :]] * (2 * count // LANES), axis=1)
        scaled = scaled.astype(jnp.bfloat16).astype(jnp.float32)
        each = 16 if tile < tiles - 1 else 8
        at = tile // 2 * 16
        some = LANES // each
        first = tile % 2 * some if tile < tiles - 1 else 0
        spec = spec.reshape(some, each, 2 * count)
        scaled = scaled.reshape(some, each, 2 * count)
        plain[first : first + some, at : at + each, :] = spec
        weighted[first : first + some, at : at + each, :] = scaled
        if first == 0:
            weighted[16:24, at : at + each, :] = scaled[:8]
    depth = plain.shape[1]

    def block(b, last):
        for lane in range(0, count, LANES):
            re = plain[b, :, lane : lane + LANES]
            im = plain[b, :, count + lane : count + lane + LANES]
            for delta in range(last + 1):
                qre = weighted[b + delta, :, lane : lane + LANES]
                qim = weighted[b + delta, :, count + lane : count + lane + LANES]
                real = (re * qre + im * qim).reshape(depth // 8, 8, LANES)
                where = delta if delta < 8 else 15
                sums[where * 16 + b, :, lane : lane + LANES] = jnp.sum(real, axis=0)
                if delta:
                    imag = (re * qim - im * qre).reshape(depth // 8, 8, LANES)
                    offset = (delta + 7) * 16 if delta < 8 else 15 * 16 + 8
                    sums[offset + b, :, lane : lane + LANES] = jnp.sum(imag, axis=0)

    lax.fori_loop(0, 8, lambda b, carry: (block(b, 8), carry)[1], 0)
    lax.fori_loop(8, 16, lambda b, carry: (block(b, 7), carry)[1], 0)
    sel = lax.broadcasted_iota(jnp.int32, (32, 256), 1) // 8
    sel = (sel == lax.broadcasted_iota(jnp.int32, (32, 256), 0)).astype(jnp.bfloat16)
    for j in range(8):
        hi, lo = split2(sums[j * 32 : (j + 1) * 32].reshape(256, count))
        part = jnp.dot(sel, hi, preferred_element_type=jnp.float32)
        part += jnp.dot(sel, lo, preferred_element_type=jnp.float32)
        high[j * 32 : (j + 1) * 32, :], low[j * 32 : (j + 1) * 32, :] = split2(part)
    half = keep_ref.shape[0]
    for ref, at in ((send_ref, half), (keep_ref, 0)):
        rows = slot_ref[at : at + half, :]
        dims = (((1,), (1,)), ((), ()))
        ref[...] = lax.dot_general(
            rows, high[...], dims, preferred_element_type=jnp.float32
        ) + lax.dot_general(rows, low[...], dims, preferred_element_type=jnp.float32)


def gram_sums(by_point, table, row_weights, slots):
    count = table.shape[1] // 2
    depth = by_point.shape[2] // 16
    vmem = pl.BlockSpec(memory_space=pltpu.VMEM)
    half = jax.ShapeDtypeStruct((slots.shape[0] // 2, 256), jnp.float32)
    return pl.pallas_call(
        gram_body,
        out_shape=(half, half),
        in_specs=[vmem] * 4,
        out_specs=(vmem, vmem),
        scratch_shapes=[
            pltpu.VMEM((16, depth, 2 * count), jnp.float32),
            pltpu.VMEM((24, depth, 2 * count), jnp.float32),
            pltpu.VMEM((256, 8, count), jnp.float32),
            pltpu.VMEM((256, count), jnp.bfloat16),
            pltpu.VMEM((256, count), jnp.bfloat16),
        ],
        compiler_params=pltpu.CompilerParams(vmem_limit_bytes=24 * 1024 * 1024),
        name="gram_sums",
    )(by_point, table, row_weights, slots)


def unpack_matrix(blocks):
    table = np.zeros((256, 2 * blocks * blocks), np.float32)
    half = blocks // 2
    for b in range(blocks):
        for e in range(blocks):
            delta = (e - b) % blocks
            if delta < half:
                real, imag, sign = 16 * delta + b, 16 * (delta + 7) + b, 1.0
            elif delta == half:
                real, imag, sign = 240 + b % half, 248 + b % half, 1.0 if b < half else -1.0
            else:
                back = blocks - delta
                real, imag, sign = 16 * back + e, 16 * (back + 7) + e, -1.0
            table[real, b * blocks + e] = 1.0
            if delta:
                table[imag, blocks * blocks + b * blocks + e] = sign
    return table


def shards(snapshots, weights, freq_bins, bin_owners):
    blocks, local_steps, fields, points = snapshots.shape
    tm_count = lax.axis_size("tm")
    pts_count = lax.axis_size("pts")
    fft_len = local_steps * tm_count
    sub_points = points // tm_count
    sent = scatter_points(jnp.transpose(snapshots, (0, 2, 1, 3)))
    by_point = lax.all_to_all(sent, "tm", split_axis=0, concat_axis=0, tiled=True)
    table = dft_columns(freq_bins, fft_len)
    slots = slot_rows(bin_owners, tm_count, lax.axis_index("pts") & 1)
    mine = lax.dynamic_slice(weights, (0, lax.axis_index("tm") * sub_points), (fields, sub_points))
    paired = jnp.broadcast_to(
        mine[: fields - 1].reshape(fields // 2, 1, 2, sub_points),
        (fields // 2, blocks, 2, sub_points),
    )
    single = jnp.broadcast_to(mine[fields - 1 :], (blocks, sub_points))
    row_weights = jnp.concatenate([paired.reshape(-1), single.reshape(-1)])
    row_weights = jnp.broadcast_to(row_weights[:, None], (row_weights.shape[0], LANES))
    keep, send = gram_sums(by_point, table, row_weights, slots)
    pairs = [(i, i ^ 1) for i in range(pts_count)]
    partial = (keep + lax.ppermute(send, "pts", pairs)).reshape(tm_count, CAP // 2, 256)
    partial = lax.all_to_all(partial, "tm", split_axis=0, concat_axis=0, tiled=True)
    owned = jnp.sum(partial, axis=0)
    copies = jnp.broadcast_to(owned[None], (pts_count,) + owned.shape)
    copies = lax.all_to_all(copies, "pts", split_axis=0, concat_axis=0, tiled=True)
    summed = jnp.sum(copies.reshape(pts_count // 2, CAP, 256), axis=0)
    return jnp.dot(
        summed, jnp.asarray(unpack_matrix(blocks)), precision=lax.Precision.HIGHEST
    )


def solution(mesh):
    in_specs = (P(None, "tm", None, "pts"), P(None, "pts"), P(), P())
    out_specs = P("tm", None)
    return jax.shard_map(shards, mesh=mesh, in_specs=in_specs, out_specs=out_specs, check_vma=False)
```

```python
import functools

import jax
import jax.numpy as jnp
import numpy as np
from jax import lax
from jax.experimental import pallas as pl
from jax.experimental.pallas import tpu as pltpu
from jax.sharding import PartitionSpec as P

CAP = 16
LANES = 128
FIRST_POINTS = 18
FIRST_SLOTS = 18
FIRST_SUMS = 14


def exchange(value, axis, first):
    size = lax.axis_size(axis)
    order = [[(c + first) % size for c in range(size)]]
    return lax.all_to_all(
        value, axis, split_axis=0, concat_axis=0, tiled=True, axis_index_groups=order
    )


def dft_columns(bin_values, fft_len, first_step):
    steps_t = (jnp.arange(fft_len, dtype=jnp.int32)[:, None] + first_step) % fft_len
    wound = bin_values[None, :] * steps_t % fft_len
    angles = 2.0 * jnp.pi * wound.astype(jnp.float32) / fft_len
    hann_window = 0.5 - 0.5 * jnp.cos(2.0 * jnp.pi * steps_t.astype(jnp.float32) / fft_len)
    scaled = hann_window / jnp.sqrt(jnp.float32(3.0 * fft_len / 8.0))
    cosine = (scaled * jnp.cos(angles)).astype(jnp.bfloat16)
    sine_rows = (-scaled * jnp.sin(angles)).astype(jnp.bfloat16)
    return jnp.concatenate([cosine, sine_rows], axis=1)


def slot_rows(bin_owners, owner_count, core):
    count = bin_owners.shape[0]
    listed = jnp.arange(count, dtype=jnp.int32)
    same = (bin_owners[:, None] == bin_owners[None, :]) & (listed[None, :] < listed[:, None])
    position = jnp.sum(same.astype(jnp.int32), axis=1)
    part = CAP // 2
    side = position // part
    row = (side != core).astype(jnp.int32) * (owner_count * part)
    place = (bin_owners + owner_count - FIRST_SLOTS) % owner_count
    row = row + place * part + position % part
    return (jnp.arange(owner_count * CAP, dtype=jnp.int32)[:, None] == row[None, :]).astype(
        jnp.bfloat16
    )


def lane_tiles(blocks, fields):
    tiles = []
    for pair in range(fields // 2):
        for first in range(0, blocks, 8):
            tiles.append([(first + g // 2, 2 * pair + g % 2) for g in range(16)])
    return tiles + [[(g, fields - 1) for g in range(16)]]


def scatter_body(x_ref, out_ref, held, ready, arrived, left):
    blocks, fields, steps, points = x_ref.shape
    groups = 16
    width = LANES // groups
    group = lax.broadcasted_iota(jnp.int32, (steps, LANES), 1) // width
    tiles = lane_tiles(blocks, fields)
    copies = []
    for tile, source in enumerate(tiles):
        firsts, lasts = source[0], source[-1]
        part = (slice(firsts[0], lasts[0] + 1), slice(firsts[1], lasts[1] + 1))
        copies.append(pltpu.make_async_copy(x_ref.at[part], held.at[part], arrived.at[tile]))
        copies[-1].start()
    for tile, source in enumerate(tiles):
        copies[tile].wait()
        for h in range(points // LANES):
            rows = []
            for g, (b, f) in enumerate(source):
                row = held[b, f, :, h * LANES : (h + 1) * LANES]
                rows.append(pltpu.roll(row, width * g, 1) if g else row)
            bit = 1
            while bit < groups:
                take = (group & bit) != 0
                rows = [jnp.where(take, rows[(c + bit) % groups], rows[c]) for c in range(groups)]
                bit *= 2
            for d in range(groups):
                row = rows[(groups - d) % groups]
                if d:
                    row = pltpu.roll(row, LANES - width * d, 1)
                ready[tile, (h * groups + d - FIRST_POINTS) % (points // 8)] = row
        lanes = slice(tile * LANES, (tile + 1) * LANES)
        copies[tile] = pltpu.make_async_copy(ready.at[tile], out_ref.at[:, :, lanes], left.at[tile])
        copies[tile].start()
    for copy in copies:
        copy.wait()


def scatter_points(x):
    blocks, fields, steps, points = x.shape
    tiles = len(lane_tiles(blocks, fields))
    wide = tiles * LANES
    return pl.pallas_call(
        scatter_body,
        out_shape=jax.ShapeDtypeStruct((points // 8, steps, wide), jnp.bfloat16),
        in_specs=[pl.BlockSpec(memory_space=pltpu.HBM)],
        out_specs=pl.BlockSpec(memory_space=pltpu.HBM),
        scratch_shapes=[
            pltpu.VMEM(x.shape, jnp.bfloat16),
            pltpu.VMEM((tiles, points // 8, steps, LANES), jnp.bfloat16),
            pltpu.SemaphoreType.DMA((tiles,)),
            pltpu.SemaphoreType.DMA((tiles,)),
        ],
        name="scatter_points",
    )(x)


def split2(value):
    high = value.astype(jnp.bfloat16)
    return high, (value - high.astype(jnp.float32)).astype(jnp.bfloat16)


def gram_body(x_ref, table_ref, w_ref, slot_ref, keep_ref, send_ref, plain, weighted, sums, high, low):
    steps = x_ref.shape[0] * x_ref.shape[1]
    count = table_ref.shape[1] // 2
    tiles = x_ref.shape[2] // LANES
    for tile in range(tiles):
        cols = slice(tile * LANES, (tile + 1) * LANES)
        spec = lax.dot_general(
            x_ref[:, :, cols].reshape(steps, LANES),
            table_ref[...],
            (((0,), (0,)), ((), ())),
            preferred_element_type=jnp.float32,
        )
        spec = spec.astype(jnp.bfloat16).astype(jnp.float32)
        scaled = spec * jnp.concatenate([w_ref[cols, :]] * (2 * count // LANES), axis=1)
        scaled = scaled.astype(jnp.bfloat16).astype(jnp.float32)
        each = 16 if tile < tiles - 1 else 8
        at = tile // 2 * 16
        some = LANES // each
        first = tile % 2 * some if tile < tiles - 1 else 0
        spec = spec.reshape(some, each, 2 * count)
        scaled = scaled.reshape(some, each, 2 * count)
        plain[first : first + some, at : at + each, :] = spec
        weighted[first : first + some, at : at + each, :] = scaled
        if first == 0:
            weighted[16:24, at : at + each, :] = scaled[:8]
    depth = plain.shape[1]

    def block(b, last):
        for lane in range(0, count, LANES):
            re = plain[b, :, lane : lane + LANES]
            im = plain[b, :, count + lane : count + lane + LANES]
            for delta in range(last + 1):
                qre = weighted[b + delta, :, lane : lane + LANES]
                qim = weighted[b + delta, :, count + lane : count + lane + LANES]
                real = (re * qre + im * qim).reshape(depth // 8, 8, LANES)
                where = delta if delta < 8 else 15
                sums[where * 16 + b, :, lane : lane + LANES] = jnp.sum(real, axis=0)
                if delta:
                    imag = (re * qim - im * qre).reshape(depth // 8, 8, LANES)
                    offset = (delta + 7) * 16 if delta < 8 else 15 * 16 + 8
                    sums[offset + b, :, lane : lane + LANES] = jnp.sum(imag, axis=0)

    lax.fori_loop(0, 8, lambda b, carry: (block(b, 8), carry)[1], 0)
    lax.fori_loop(8, 16, lambda b, carry: (block(b, 7), carry)[1], 0)
    sel = lax.broadcasted_iota(jnp.int32, (32, 256), 1) // 8
    sel = (sel == lax.broadcasted_iota(jnp.int32, (32, 256), 0)).astype(jnp.bfloat16)
    for j in range(8):
        hi, lo = split2(sums[j * 32 : (j + 1) * 32].reshape(256, count))
        part = jnp.dot(sel, hi, preferred_element_type=jnp.float32)
        part += jnp.dot(sel, lo, preferred_element_type=jnp.float32)
        high[j * 32 : (j + 1) * 32, :], low[j * 32 : (j + 1) * 32, :] = split2(part)
    half = keep_ref.shape[0]
    for ref, at in ((send_ref, half), (keep_ref, 0)):
        rows = slot_ref[at : at + half, :]
        dims = (((1,), (1,)), ((), ()))
        ref[...] = lax.dot_general(
            rows, high[...], dims, preferred_element_type=jnp.float32
        ) + lax.dot_general(rows, low[...], dims, preferred_element_type=jnp.float32)


def gram_sums(by_point, table, row_weights, slots):
    count = table.shape[1] // 2
    depth = by_point.shape[2] // 16
    vmem = pl.BlockSpec(memory_space=pltpu.VMEM)
    half = jax.ShapeDtypeStruct((slots.shape[0] // 2, 256), jnp.float32)
    return pl.pallas_call(
        gram_body,
        out_shape=(half, half),
        in_specs=[vmem] * 4,
        out_specs=(vmem, vmem),
        scratch_shapes=[
            pltpu.VMEM((16, depth, 2 * count), jnp.float32),
            pltpu.VMEM((24, depth, 2 * count), jnp.float32),
            pltpu.VMEM((256, 8, count), jnp.float32),
            pltpu.VMEM((256, count), jnp.bfloat16),
            pltpu.VMEM((256, count), jnp.bfloat16),
        ],
        compiler_params=pltpu.CompilerParams(vmem_limit_bytes=24 * 1024 * 1024),
        name="gram_sums",
    )(by_point, table, row_weights, slots)


def unpack_matrix(blocks):
    table = np.zeros((256, 2 * blocks * blocks), np.float32)
    half = blocks // 2
    for b in range(blocks):
        for e in range(blocks):
            delta = (e - b) % blocks
            if delta < half:
                real, imag, sign = 16 * delta + b, 16 * (delta + 7) + b, 1.0
            elif delta == half:
                real, imag, sign = 240 + b % half, 248 + b % half, 1.0 if b < half else -1.0
            else:
                back = blocks - delta
                real, imag, sign = 16 * back + e, 16 * (back + 7) + e, -1.0
            table[real, b * blocks + e] = 1.0
            if delta:
                table[imag, blocks * blocks + b * blocks + e] = sign
    return table


def shards(snapshots, weights, freq_bins, bin_owners):
    blocks, local_steps, fields, points = snapshots.shape
    tm_count = lax.axis_size("tm")
    pts_count = lax.axis_size("pts")
    fft_len = local_steps * tm_count
    sub_points = points // tm_count
    sent = scatter_points(jnp.transpose(snapshots, (0, 2, 1, 3)))
    by_point = exchange(sent, "tm", FIRST_POINTS)
    table = dft_columns(freq_bins, fft_len, FIRST_POINTS * local_steps)
    slots = slot_rows(bin_owners, tm_count, lax.axis_index("pts") & 1)
    mine = lax.dynamic_slice(weights, (0, lax.axis_index("tm") * sub_points), (fields, sub_points))
    paired = jnp.broadcast_to(
        mine[: fields - 1].reshape(fields // 2, 1, 2, sub_points),
        (fields // 2, blocks, 2, sub_points),
    )
    single = jnp.broadcast_to(mine[fields - 1 :], (blocks, sub_points))
    row_weights = jnp.concatenate([paired.reshape(-1), single.reshape(-1)])
    row_weights = jnp.broadcast_to(row_weights[:, None], (row_weights.shape[0], LANES))
    keep, send = gram_sums(by_point, table, row_weights, slots)
    pairs = [(i, i ^ 1) for i in range(pts_count)]
    partial = (keep + lax.ppermute(send, "pts", pairs)).reshape(tm_count, CAP // 2, 256)
    partial = exchange(partial, "tm", FIRST_SLOTS)
    owned = jnp.sum(partial, axis=0)
    copies = jnp.broadcast_to(owned[None], (pts_count,) + owned.shape)
    copies = exchange(copies, "pts", FIRST_SUMS)
    summed = jnp.sum(copies.reshape(pts_count // 2, CAP, 256), axis=0)
    return jnp.dot(
        summed, jnp.asarray(unpack_matrix(blocks)), precision=lax.Precision.HIGHEST
    )


def solution(mesh):
    in_specs = (P(None, "tm", None, "pts"), P(None, "pts"), P(), P())
    out_specs = P("tm", None)
    return jax.shard_map(shards, mesh=mesh, in_specs=in_specs, out_specs=out_specs, check_vma=False)
```

```python
import functools

import jax
import jax.numpy as jnp
import numpy as np
from jax import lax
from jax.experimental import pallas as pl
from jax.experimental.pallas import tpu as pltpu
from jax.sharding import PartitionSpec as P

CAP = 16
LANES = 128
FIRST_POINTS = 18
FIRST_SLOTS = 18
FIRST_SUMS = 12


def exchange(value, axis, first):
    size = lax.axis_size(axis)
    order = [[(c + first) % size for c in range(size)]]
    return lax.all_to_all(
        value, axis, split_axis=0, concat_axis=0, tiled=True, axis_index_groups=order
    )


def dft_columns(bin_values, fft_len, first_step):
    steps_t = (jnp.arange(fft_len, dtype=jnp.int32)[:, None] + first_step) % fft_len
    wound = bin_values[None, :] * steps_t % fft_len
    angles = 2.0 * jnp.pi * wound.astype(jnp.float32) / fft_len
    hann_window = 0.5 - 0.5 * jnp.cos(2.0 * jnp.pi * steps_t.astype(jnp.float32) / fft_len)
    scaled = hann_window / jnp.sqrt(jnp.float32(3.0 * fft_len / 8.0))
    cosine = (scaled * jnp.cos(angles)).astype(jnp.bfloat16)
    sine_rows = (-scaled * jnp.sin(angles)).astype(jnp.bfloat16)
    return jnp.concatenate([cosine, sine_rows], axis=1)


def slot_rows(bin_owners, owner_count, core):
    count = bin_owners.shape[0]
    listed = jnp.arange(count, dtype=jnp.int32)
    same = (bin_owners[:, None] == bin_owners[None, :]) & (listed[None, :] < listed[:, None])
    position = jnp.sum(same.astype(jnp.int32), axis=1)
    part = CAP // 2
    side = position // part
    row = (side != core).astype(jnp.int32) * (owner_count * part)
    place = (bin_owners + owner_count - FIRST_SLOTS) % owner_count
    row = row + place * part + position % part
    return (jnp.arange(owner_count * CAP, dtype=jnp.int32)[:, None] == row[None, :]).astype(
        jnp.bfloat16
    )


def lane_tiles(blocks, fields):
    tiles = []
    for pair in range(fields // 2):
        for first in range(0, blocks, 8):
            tiles.append([(first + g // 2, 2 * pair + g % 2) for g in range(16)])
    return tiles + [[(g, fields - 1) for g in range(16)]]


def scatter_body(x_ref, out_ref, held, ready, arrived, left):
    blocks, fields, steps, points = x_ref.shape
    groups = 16
    width = LANES // groups
    group = lax.broadcasted_iota(jnp.int32, (steps, LANES), 1) // width
    tiles = lane_tiles(blocks, fields)
    copies = []
    for tile, source in enumerate(tiles):
        firsts, lasts = source[0], source[-1]
        part = (slice(firsts[0], lasts[0] + 1), slice(firsts[1], lasts[1] + 1))
        copies.append(pltpu.make_async_copy(x_ref.at[part], held.at[part], arrived.at[tile]))
        copies[-1].start()
    for tile, source in enumerate(tiles):
        copies[tile].wait()
        for h in range(points // LANES):
            rows = []
            for g, (b, f) in enumerate(source):
                row = held[b, f, :, h * LANES : (h + 1) * LANES]
                rows.append(pltpu.roll(row, width * g, 1) if g else row)
            bit = 1
            while bit < groups:
                take = (group & bit) != 0
                rows = [jnp.where(take, rows[(c + bit) % groups], rows[c]) for c in range(groups)]
                bit *= 2
            for d in range(groups):
                ready[tile, (h * groups + d - FIRST_POINTS) % (points // 8)] = rows[
                    (groups - d) % groups
                ]
        lanes = slice(tile * LANES, (tile + 1) * LANES)
        copies[tile] = pltpu.make_async_copy(ready.at[tile], out_ref.at[:, :, lanes], left.at[tile])
        copies[tile].start()
    for copy in copies:
        copy.wait()


def scatter_points(x):
    blocks, fields, steps, points = x.shape
    tiles = len(lane_tiles(blocks, fields))
    wide = tiles * LANES
    return pl.pallas_call(
        scatter_body,
        out_shape=jax.ShapeDtypeStruct((points // 8, steps, wide), jnp.bfloat16),
        in_specs=[pl.BlockSpec(memory_space=pltpu.HBM)],
        out_specs=pl.BlockSpec(memory_space=pltpu.HBM),
        scratch_shapes=[
            pltpu.VMEM(x.shape, jnp.bfloat16),
            pltpu.VMEM((tiles, points // 8, steps, LANES), jnp.bfloat16),
            pltpu.SemaphoreType.DMA((tiles,)),
            pltpu.SemaphoreType.DMA((tiles,)),
        ],
        name="scatter_points",
    )(x)


def split2(value):
    high = value.astype(jnp.bfloat16)
    return high, (value - high.astype(jnp.float32)).astype(jnp.bfloat16)


def gram_body(x_ref, table_ref, w_ref, slot_ref, keep_ref, send_ref, plain, weighted, sums, high, low):
    steps = x_ref.shape[0] * x_ref.shape[1]
    count = table_ref.shape[1] // 2
    tiles = x_ref.shape[2] // LANES
    turn = lax.axis_index("tm") % 16
    for tile in range(tiles):
        cols = slice(tile * LANES, (tile + 1) * LANES)
        spec = lax.dot_general(
            x_ref[:, :, cols].reshape(steps, LANES),
            table_ref[...],
            (((0,), (0,)), ((), ())),
            preferred_element_type=jnp.float32,
        )
        spec = spec.astype(jnp.bfloat16).astype(jnp.float32)
        for g in range(16):
            source = (g - turn + 16) % 16
            if tile < tiles - 1:
                b, f = tile % 2 * 8 + source // 2, tile // 2 * 2 + source % 2
            else:
                b, f = source, tiles - 1
            at = pl.ds(pl.multiple_of(f * 8, 8), 8)
            piece = spec[g * 8 : (g + 1) * 8, :]
            scaled = piece * jnp.concatenate([w_ref[at, :]] * (2 * count // LANES), axis=1)
            plain[b, at, :] = piece
            weighted[b, at, :] = scaled.astype(jnp.bfloat16).astype(jnp.float32)
    depth = plain.shape[1]

    def block(b, last):
        for lane in range(0, count, LANES):
            re = plain[b, :, lane : lane + LANES]
            im = plain[b, :, count + lane : count + lane + LANES]
            for delta in range(last + 1):
                e = (b + delta) % 16
                qre = weighted[e, :, lane : lane + LANES]
                qim = weighted[e, :, count + lane : count + lane + LANES]
                real = (re * qre + im * qim).reshape(depth // 8, 8, LANES)
                where = delta if delta < 8 else 15
                sums[where * 16 + b, :, lane : lane + LANES] = jnp.sum(real, axis=0)
                if delta:
                    imag = (re * qim - im * qre).reshape(depth // 8, 8, LANES)
                    offset = (delta + 7) * 16 if delta < 8 else 15 * 16 + 8
                    sums[offset + b, :, lane : lane + LANES] = jnp.sum(imag, axis=0)

    lax.fori_loop(0, 8, lambda b, carry: (block(b, 8), carry)[1], 0)
    lax.fori_loop(8, 16, lambda b, carry: (block(b, 7), carry)[1], 0)
    sel = lax.broadcasted_iota(jnp.int32, (32, 256), 1) // 8
    sel = (sel == lax.broadcasted_iota(jnp.int32, (32, 256), 0)).astype(jnp.bfloat16)
    for j in range(8):
        hi, lo = split2(sums[j * 32 : (j + 1) * 32].reshape(256, count))
        part = jnp.dot(sel, hi, preferred_element_type=jnp.float32)
        part += jnp.dot(sel, lo, preferred_element_type=jnp.float32)
        high[j * 32 : (j + 1) * 32, :], low[j * 32 : (j + 1) * 32, :] = split2(part)
    half = keep_ref.shape[0]
    for ref, at in ((send_ref, half), (keep_ref, 0)):
        rows = slot_ref[at : at + half, :]
        dims = (((1,), (1,)), ((), ()))
        ref[...] = lax.dot_general(
            rows, high[...], dims, preferred_element_type=jnp.float32
        ) + lax.dot_general(rows, low[...], dims, preferred_element_type=jnp.float32)


def gram_sums(by_point, table, row_weights, slots):
    count = table.shape[1] // 2
    depth = by_point.shape[2] // 16
    vmem = pl.BlockSpec(memory_space=pltpu.VMEM)
    half = jax.ShapeDtypeStruct((slots.shape[0] // 2, 256), jnp.float32)
    return pl.pallas_call(
        gram_body,
        out_shape=(half, half),
        in_specs=[vmem] * 4,
        out_specs=(vmem, vmem),
        scratch_shapes=[
            pltpu.VMEM((16, depth, 2 * count), jnp.float32),
            pltpu.VMEM((16, depth, 2 * count), jnp.float32),
            pltpu.VMEM((256, 8, count), jnp.float32),
            pltpu.VMEM((256, count), jnp.bfloat16),
            pltpu.VMEM((256, count), jnp.bfloat16),
        ],
        compiler_params=pltpu.CompilerParams(vmem_limit_bytes=24 * 1024 * 1024),
        name="gram_sums",
    )(by_point, table, row_weights, slots)


def unpack_matrix(blocks):
    table = np.zeros((256, 2 * blocks * blocks), np.float32)
    half = blocks // 2
    for b in range(blocks):
        for e in range(blocks):
            delta = (e - b) % blocks
            if delta < half:
                real, imag, sign = 16 * delta + b, 16 * (delta + 7) + b, 1.0
            elif delta == half:
                real, imag, sign = 240 + b % half, 248 + b % half, 1.0 if b < half else -1.0
            else:
                back = blocks - delta
                real, imag, sign = 16 * back + e, 16 * (back + 7) + e, -1.0
            table[real, b * blocks + e] = 1.0
            if delta:
                table[imag, blocks * blocks + b * blocks + e] = sign
    return table


def shards(snapshots, weights, freq_bins, bin_owners):
    blocks, local_steps, fields, points = snapshots.shape
    tm_count = lax.axis_size("tm")
    pts_count = lax.axis_size("pts")
    fft_len = local_steps * tm_count
    sub_points = points // tm_count
    sent = scatter_points(jnp.transpose(snapshots, (0, 2, 1, 3)))
    by_point = exchange(sent, "tm", FIRST_POINTS)
    table = dft_columns(freq_bins, fft_len, FIRST_POINTS * local_steps)
    slots = slot_rows(bin_owners, tm_count, lax.axis_index("pts") & 1)
    mine = lax.dynamic_slice(weights, (0, lax.axis_index("tm") * sub_points), (fields, sub_points))
    row_weights = jnp.broadcast_to(mine[:, :, None], (fields, sub_points, LANES))
    row_weights = row_weights.reshape(fields * sub_points, LANES)
    keep, send = gram_sums(by_point, table, row_weights, slots)
    pairs = [(i, i ^ 1) for i in range(pts_count)]
    partial = (keep + lax.ppermute(send, "pts", pairs)).reshape(tm_count, CAP // 2, 256)
    partial = exchange(partial, "tm", FIRST_SLOTS)
    owned = jnp.sum(partial, axis=0)
    copies = jnp.broadcast_to(owned[None], (pts_count,) + owned.shape)
    copies = exchange(copies, "pts", FIRST_SUMS)
    summed = jnp.sum(copies.reshape(pts_count // 2, CAP, 256), axis=0)
    return jnp.dot(
        summed, jnp.asarray(unpack_matrix(blocks)), precision=lax.Precision.HIGHEST
    )


def solution(mesh):
    in_specs = (P(None, "tm", None, "pts"), P(None, "pts"), P(), P())
    out_specs = P("tm", None)
    return jax.shard_map(shards, mesh=mesh, in_specs=in_specs, out_specs=out_specs, check_vma=False)
```

```python
import functools

import jax
import jax.numpy as jnp
import numpy as np
from jax import lax
from jax.experimental import pallas as pl
from jax.experimental.pallas import tpu as pltpu
from jax.sharding import PartitionSpec as P

CAP = 16
LANES = 128
FIRST_POINTS = 18
FIRST_SLOTS = 18
FIRST_SUMS = 12


def exchange(value, axis, first):
    size = lax.axis_size(axis)
    order = [[(c + first) % size for c in range(size)]]
    return lax.all_to_all(
        value, axis, split_axis=0, concat_axis=0, tiled=True, axis_index_groups=order
    )


def dft_columns(bin_values, fft_len, first_step):
    steps_t = (jnp.arange(fft_len, dtype=jnp.int32)[:, None] + first_step) % fft_len
    wound = bin_values[None, :] * steps_t % fft_len
    angles = 2.0 * jnp.pi * wound.astype(jnp.float32) / fft_len
    hann_window = 0.5 - 0.5 * jnp.cos(2.0 * jnp.pi * steps_t.astype(jnp.float32) / fft_len)
    scaled = hann_window / jnp.sqrt(jnp.float32(3.0 * fft_len / 8.0))
    cosine = (scaled * jnp.cos(angles)).astype(jnp.bfloat16)
    sine_rows = (-scaled * jnp.sin(angles)).astype(jnp.bfloat16)
    return jnp.concatenate([cosine, sine_rows], axis=1)


def slot_rows(bin_owners, owner_count, core):
    count = bin_owners.shape[0]
    listed = jnp.arange(count, dtype=jnp.int32)
    same = (bin_owners[:, None] == bin_owners[None, :]) & (listed[None, :] < listed[:, None])
    position = jnp.sum(same.astype(jnp.int32), axis=1)
    part = CAP // 2
    side = position // part
    row = (side != core).astype(jnp.int32) * (owner_count * part)
    place = (bin_owners + owner_count - FIRST_SLOTS) % owner_count
    row = row + place * part + position % part
    return (jnp.arange(owner_count * CAP, dtype=jnp.int32)[:, None] == row[None, :]).astype(
        jnp.bfloat16
    )


def lane_tiles(blocks, fields):
    tiles = []
    for pair in range(fields // 2):
        for first in range(0, blocks, 8):
            tiles.append([(first + g // 2, 2 * pair + g % 2) for g in range(16)])
    return tiles + [[(g, fields - 1) for g in range(16)]]


def scatter_body(x_ref, out_ref, held, ready, arrived, left):
    blocks, fields, steps, points = x_ref.shape
    groups = 16
    width = LANES // groups
    group = lax.broadcasted_iota(jnp.int32, (steps, LANES), 1) // width
    tiles = lane_tiles(blocks, fields)
    copies = []
    for tile, source in enumerate(tiles):
        firsts, lasts = source[0], source[-1]
        part = (slice(firsts[0], lasts[0] + 1), slice(firsts[1], lasts[1] + 1))
        copies.append(pltpu.make_async_copy(x_ref.at[part], held.at[part], arrived.at[tile]))
        copies[-1].start()
    for tile, source in enumerate(tiles):
        copies[tile].wait()
        for h in range(points // LANES):
            rows = []
            for g, (b, f) in enumerate(source):
                row = held[b, f, :, h * LANES : (h + 1) * LANES]
                rows.append(pltpu.roll(row, width * g, 1) if g else row)
            bit = 1
            while bit < groups:
                take = (group & bit) != 0
                rows = [jnp.where(take, rows[(c + bit) % groups], rows[c]) for c in range(groups)]
                bit *= 2
            for d in range(groups):
                ready[tile, (h * groups + d - FIRST_POINTS) % (points // 8)] = rows[
                    (groups - d) % groups
                ]
        lanes = slice(tile * LANES, (tile + 1) * LANES)
        copies[tile] = pltpu.make_async_copy(ready.at[tile], out_ref.at[:, :, lanes], left.at[tile])
        copies[tile].start()
    for copy in copies:
        copy.wait()


def scatter_points(x):
    blocks, fields, steps, points = x.shape
    tiles = len(lane_tiles(blocks, fields))
    wide = tiles * LANES
    return pl.pallas_call(
        scatter_body,
        out_shape=jax.ShapeDtypeStruct((points // 8, steps, wide), jnp.bfloat16),
        in_specs=[pl.BlockSpec(memory_space=pltpu.HBM)],
        out_specs=pl.BlockSpec(memory_space=pltpu.HBM),
        scratch_shapes=[
            pltpu.VMEM(x.shape, jnp.bfloat16),
            pltpu.VMEM((tiles, points // 8, steps, LANES), jnp.bfloat16),
            pltpu.SemaphoreType.DMA((tiles,)),
            pltpu.SemaphoreType.DMA((tiles,)),
        ],
        name="scatter_points",
    )(x)


def split2(value):
    high = value.astype(jnp.bfloat16)
    return high, (value - high.astype(jnp.float32)).astype(jnp.bfloat16)


def gram_body(x_ref, table_ref, w_ref, slot_ref, keep_ref, send_ref, plain, weighted, sums, high, low):
    steps = x_ref.shape[0] * x_ref.shape[1]
    count = table_ref.shape[1] // 2
    tiles = x_ref.shape[2] // LANES
    turn = lax.axis_index("tm") % 16
    for tile in range(tiles):
        cols = slice(tile * LANES, (tile + 1) * LANES)
        spec = lax.dot_general(
            x_ref[:, :, cols].reshape(steps, LANES),
            table_ref[...],
            (((0,), (0,)), ((), ())),
            preferred_element_type=jnp.float32,
        )
        spec = spec.astype(jnp.bfloat16).astype(jnp.float32)
        for g in range(16):
            source = (g - turn + 16) % 16
            if tile < tiles - 1:
                b, f = tile % 2 * 8 + source // 2, tile // 2 * 2 + source % 2
            else:
                b, f = source, tiles - 1
            at = pl.ds(pl.multiple_of(f * 8, 8), 8)
            piece = spec[g * 8 : (g + 1) * 8, :]
            scaled = piece * jnp.concatenate([w_ref[at, :]] * (2 * count // LANES), axis=1)
            plain[b, at, :] = piece
            weighted[b, at, :] = scaled.astype(jnp.bfloat16).astype(jnp.float32)
    depth = plain.shape[1]

    def block(b, last):
        for lane in range(0, count, LANES):
            re = plain[b, :, lane : lane + LANES]
            im = plain[b, :, count + lane : count + lane + LANES]
            for delta in range(last + 1):
                e = (b + delta) % 16
                qre = weighted[e, :, lane : lane + LANES]
                qim = weighted[e, :, count + lane : count + lane + LANES]
                real = (re * qre + im * qim).reshape(depth // 8, 8, LANES)
                where = delta if delta < 8 else 15
                sums[where * 16 + b, :, lane : lane + LANES] = jnp.sum(real, axis=0)
                if delta:
                    imag = (re * qim - im * qre).reshape(depth // 8, 8, LANES)
                    offset = (delta + 7) * 16 if delta < 8 else 15 * 16 + 8
                    sums[offset + b, :, lane : lane + LANES] = jnp.sum(imag, axis=0)

    lax.fori_loop(0, 8, lambda b, carry: (block(b, 8), carry)[1], 0)
    lax.fori_loop(8, 16, lambda b, carry: (block(b, 7), carry)[1], 0)
    sel = lax.broadcasted_iota(jnp.int32, (32, 256), 1) // 8
    sel = (sel == lax.broadcasted_iota(jnp.int32, (32, 256), 0)).astype(jnp.bfloat16)
    for j in range(8):
        hi, lo = split2(sums[j * 32 : (j + 1) * 32].reshape(256, count))
        part = jnp.dot(sel, hi, preferred_element_type=jnp.float32)
        part += jnp.dot(sel, lo, preferred_element_type=jnp.float32)
        high[j * 32 : (j + 1) * 32, :], low[j * 32 : (j + 1) * 32, :] = split2(part)
    half = keep_ref.shape[0]
    for ref, at in ((send_ref, half), (keep_ref, 0)):
        rows = slot_ref[at : at + half, :]
        dims = (((1,), (1,)), ((), ()))
        ref[...] = lax.dot_general(
            rows, high[...], dims, preferred_element_type=jnp.float32
        ) + lax.dot_general(rows, low[...], dims, preferred_element_type=jnp.float32)


def gram_sums(by_point, table, row_weights, slots):
    count = table.shape[1] // 2
    depth = by_point.shape[2] // 16
    vmem = pl.BlockSpec(memory_space=pltpu.VMEM)
    half = jax.ShapeDtypeStruct((slots.shape[0] // 2, 256), jnp.float32)
    return pl.pallas_call(
        gram_body,
        out_shape=(half, half),
        in_specs=[vmem] * 4,
        out_specs=(vmem, vmem),
        scratch_shapes=[
            pltpu.VMEM((16, depth, 2 * count), jnp.float32),
            pltpu.VMEM((16, depth, 2 * count), jnp.float32),
            pltpu.VMEM((256, 8, count), jnp.float32),
            pltpu.VMEM((256, count), jnp.bfloat16),
            pltpu.VMEM((256, count), jnp.bfloat16),
        ],
        compiler_params=pltpu.CompilerParams(vmem_limit_bytes=24 * 1024 * 1024),
        name="gram_sums",
    )(by_point, table, row_weights, slots)


def finish_body(parts_ref, unpack_ref, out_ref):
    total = jnp.sum(parts_ref[...], axis=0)
    first = total.astype(jnp.bfloat16)
    rest = total - first.astype(jnp.float32)
    second = rest.astype(jnp.bfloat16)
    third = (rest - second.astype(jnp.float32)).astype(jnp.bfloat16)
    rows = jnp.concatenate([first, second, third], axis=0)
    full = jnp.dot(rows, unpack_ref[...], preferred_element_type=jnp.float32)
    slots = total.shape[0]
    out_ref[...] = full[:slots] + full[slots : 2 * slots] + full[2 * slots :]


def finish(parts, unpack):
    vmem = pl.BlockSpec(memory_space=pltpu.VMEM)
    return pl.pallas_call(
        finish_body,
        out_shape=jax.ShapeDtypeStruct((parts.shape[1], unpack.shape[1]), jnp.float32),
        in_specs=[vmem] * 2,
        out_specs=vmem,
        compiler_params=pltpu.CompilerParams(vmem_limit_bytes=8 * 1024 * 1024),
        name="finish",
    )(parts, unpack)


def unpack_matrix(blocks):
    table = np.zeros((256, 2 * blocks * blocks), np.float32)
    half = blocks // 2
    for b in range(blocks):
        for e in range(blocks):
            delta = (e - b) % blocks
            if delta < half:
                real, imag, sign = 16 * delta + b, 16 * (delta + 7) + b, 1.0
            elif delta == half:
                real, imag, sign = 240 + b % half, 248 + b % half, 1.0 if b < half else -1.0
            else:
                back = blocks - delta
                real, imag, sign = 16 * back + e, 16 * (back + 7) + e, -1.0
            table[real, b * blocks + e] = 1.0
            if delta:
                table[imag, blocks * blocks + b * blocks + e] = sign
    return table


def shards(snapshots, weights, freq_bins, bin_owners):
    blocks, local_steps, fields, points = snapshots.shape
    tm_count = lax.axis_size("tm")
    pts_count = lax.axis_size("pts")
    fft_len = local_steps * tm_count
    sub_points = points // tm_count
    sent = scatter_points(jnp.transpose(snapshots, (0, 2, 1, 3)))
    by_point = exchange(sent, "tm", FIRST_POINTS)
    table = dft_columns(freq_bins, fft_len, FIRST_POINTS * local_steps)
    slots = slot_rows(bin_owners, tm_count, lax.axis_index("pts") & 1)
    mine = lax.dynamic_slice(weights, (0, lax.axis_index("tm") * sub_points), (fields, sub_points))
    row_weights = jnp.broadcast_to(mine[:, :, None], (fields, sub_points, LANES))
    row_weights = row_weights.reshape(fields * sub_points, LANES)
    keep, send = gram_sums(by_point, table, row_weights, slots)
    pairs = [(i, i ^ 1) for i in range(pts_count)]
    partial = (keep + lax.ppermute(send, "pts", pairs)).reshape(tm_count, CAP // 2, 256)
    partial = exchange(partial, "tm", FIRST_SLOTS)
    owned = jnp.sum(partial, axis=0)
    copies = jnp.broadcast_to(owned[None], (pts_count,) + owned.shape)
    copies = exchange(copies, "pts", FIRST_SUMS)
    parts = copies.reshape(pts_count // 2, CAP, 256)
    return finish(parts, jnp.asarray(unpack_matrix(blocks), jnp.bfloat16))


def solution(mesh):
    in_specs = (P(None, "tm", None, "pts"), P(None, "pts"), P(), P())
    out_specs = P("tm", None)
    return jax.shard_map(shards, mesh=mesh, in_specs=in_specs, out_specs=out_specs, check_vma=False)
```

```python
import functools

import jax
import jax.numpy as jnp
import numpy as np
from jax import lax
from jax.experimental import pallas as pl
from jax.experimental.pallas import tpu as pltpu
from jax.sharding import PartitionSpec as P

CAP = 16
LANES = 128
FIRST_POINTS = 18
FIRST_SLOTS = 18
FIRST_SUMS = 10


def exchange(value, axis, first):
    size = lax.axis_size(axis)
    order = [[(c + first) % size for c in range(size)]]
    return lax.all_to_all(
        value, axis, split_axis=0, concat_axis=0, tiled=True, axis_index_groups=order
    )


def dft_columns(bin_values, fft_len, first_step):
    steps_t = (jnp.arange(fft_len, dtype=jnp.int32)[:, None] + first_step) % fft_len
    wound = bin_values[None, :] * steps_t % fft_len
    angles = 2.0 * jnp.pi * wound.astype(jnp.float32) / fft_len
    hann_window = 0.5 - 0.5 * jnp.cos(2.0 * jnp.pi * steps_t.astype(jnp.float32) / fft_len)
    scaled = hann_window / jnp.sqrt(jnp.float32(3.0 * fft_len / 8.0))
    cosine = (scaled * jnp.cos(angles)).astype(jnp.bfloat16)
    sine_rows = (-scaled * jnp.sin(angles)).astype(jnp.bfloat16)
    return jnp.concatenate([cosine, sine_rows], axis=1)


def slot_rows(bin_owners, owner_count, core):
    count = bin_owners.shape[0]
    listed = jnp.arange(count, dtype=jnp.int32)
    same = (bin_owners[:, None] == bin_owners[None, :]) & (listed[None, :] < listed[:, None])
    position = jnp.sum(same.astype(jnp.int32), axis=1)
    part = CAP // 2
    side = position // part
    row = (side != core).astype(jnp.int32) * (owner_count * part)
    place = (bin_owners + owner_count - FIRST_SLOTS) % owner_count
    row = row + place * part + position % part
    return (jnp.arange(owner_count * CAP, dtype=jnp.int32)[:, None] == row[None, :]).astype(
        jnp.bfloat16
    )


def lane_tiles(blocks, fields):
    tiles = []
    for pair in range(fields // 2):
        for first in range(0, blocks, 8):
            tiles.append([(first + g // 2, 2 * pair + g % 2) for g in range(16)])
    return tiles + [[(g, fields - 1) for g in range(16)]]


def scatter_body(x_ref, out_ref, held, ready, arrived, left):
    blocks, fields, steps, points = x_ref.shape
    groups = 16
    width = LANES // groups
    group = lax.broadcasted_iota(jnp.int32, (steps, LANES), 1) // width
    tiles = lane_tiles(blocks, fields)
    copies = []
    for tile, source in enumerate(tiles):
        firsts, lasts = source[0], source[-1]
        part = (slice(firsts[0], lasts[0] + 1), slice(firsts[1], lasts[1] + 1))
        copies.append(pltpu.make_async_copy(x_ref.at[part], held.at[part], arrived.at[tile]))
        copies[-1].start()
    for tile, source in enumerate(tiles):
        copies[tile].wait()
        for h in range(points // LANES):
            rows = []
            for g, (b, f) in enumerate(source):
                row = held[b, f, :, h * LANES : (h + 1) * LANES]
                rows.append(pltpu.roll(row, width * g, 1) if g else row)
            bit = 1
            while bit < groups:
                take = (group & bit) != 0
                rows = [jnp.where(take, rows[(c + bit) % groups], rows[c]) for c in range(groups)]
                bit *= 2
            for d in range(groups):
                ready[tile, (h * groups + d - FIRST_POINTS) % (points // 8)] = rows[
                    (groups - d) % groups
                ]
        lanes = slice(tile * LANES, (tile + 1) * LANES)
        copies[tile] = pltpu.make_async_copy(ready.at[tile], out_ref.at[:, :, lanes], left.at[tile])
        copies[tile].start()
    for copy in copies:
        copy.wait()


def scatter_points(x):
    blocks, fields, steps, points = x.shape
    tiles = len(lane_tiles(blocks, fields))
    wide = tiles * LANES
    return pl.pallas_call(
        scatter_body,
        out_shape=jax.ShapeDtypeStruct((points // 8, steps, wide), jnp.bfloat16),
        in_specs=[pl.BlockSpec(memory_space=pltpu.HBM)],
        out_specs=pl.BlockSpec(memory_space=pltpu.HBM),
        scratch_shapes=[
            pltpu.VMEM(x.shape, jnp.bfloat16),
            pltpu.VMEM((tiles, points // 8, steps, LANES), jnp.bfloat16),
            pltpu.SemaphoreType.DMA((tiles,)),
            pltpu.SemaphoreType.DMA((tiles,)),
        ],
        name="scatter_points",
    )(x)


def split2(value):
    high = value.astype(jnp.bfloat16)
    return high, (value - high.astype(jnp.float32)).astype(jnp.bfloat16)


def gram_body(x_ref, table_ref, w_ref, slot_ref, keep_ref, send_ref, plain, weighted, sums, high, low):
    steps = x_ref.shape[0] * x_ref.shape[1]
    count = table_ref.shape[1] // 2
    tiles = x_ref.shape[2] // LANES
    turn = lax.axis_index("tm") % 16
    for tile in range(tiles):
        cols = slice(tile * LANES, (tile + 1) * LANES)
        spec = lax.dot_general(
            x_ref[:, :, cols].reshape(steps, LANES),
            table_ref[...],
            (((0,), (0,)), ((), ())),
            preferred_element_type=jnp.float32,
        )
        spec = spec.astype(jnp.bfloat16).astype(jnp.float32)
        for g in range(16):
            source = (g - turn + 16) % 16
            if tile < tiles - 1:
                b, f = tile % 2 * 8 + source // 2, tile // 2 * 2 + source % 2
            else:
                b, f = source, tiles - 1
            at = pl.ds(pl.multiple_of(f * 8, 8), 8)
            piece = spec[g * 8 : (g + 1) * 8, :]
            scaled = piece * jnp.concatenate([w_ref[at, :]] * (2 * count // LANES), axis=1)
            plain[b, at, :] = piece
            weighted[b, at, :] = scaled.astype(jnp.bfloat16).astype(jnp.float32)
    depth = plain.shape[1]

    def block(b, last):
        for lane in range(0, count, LANES):
            re = plain[b, :, lane : lane + LANES]
            im = plain[b, :, count + lane : count + lane + LANES]
            for delta in range(last + 1):
                e = (b + delta) % 16
                qre = weighted[e, :, lane : lane + LANES]
                qim = weighted[e, :, count + lane : count + lane + LANES]
                real = (re * qre + im * qim).reshape(depth // 8, 8, LANES)
                where = delta if delta < 8 else 15
                sums[where * 16 + b, :, lane : lane + LANES] = jnp.sum(real, axis=0)
                if delta:
                    imag = (re * qim - im * qre).reshape(depth // 8, 8, LANES)
                    offset = (delta + 7) * 16 if delta < 8 else 15 * 16 + 8
                    sums[offset + b, :, lane : lane + LANES] = jnp.sum(imag, axis=0)

    lax.fori_loop(0, 8, lambda b, carry: (block(b, 8), carry)[1], 0)
    lax.fori_loop(8, 16, lambda b, carry: (block(b, 7), carry)[1], 0)
    sel = lax.broadcasted_iota(jnp.int32, (32, 256), 1) // 8
    sel = (sel == lax.broadcasted_iota(jnp.int32, (32, 256), 0)).astype(jnp.bfloat16)
    for j in range(8):
        hi, lo = split2(sums[j * 32 : (j + 1) * 32].reshape(256, count))
        part = jnp.dot(sel, hi, preferred_element_type=jnp.float32)
        part += jnp.dot(sel, lo, preferred_element_type=jnp.float32)
        high[j * 32 : (j + 1) * 32, :], low[j * 32 : (j + 1) * 32, :] = split2(part)
    half = keep_ref.shape[0]
    for ref, at in ((send_ref, half), (keep_ref, 0)):
        rows = slot_ref[at : at + half, :]
        dims = (((1,), (1,)), ((), ()))
        ref[...] = lax.dot_general(
            rows, high[...], dims, preferred_element_type=jnp.float32
        ) + lax.dot_general(rows, low[...], dims, preferred_element_type=jnp.float32)


def gram_sums(by_point, table, row_weights, slots):
    count = table.shape[1] // 2
    depth = by_point.shape[2] // 16
    vmem = pl.BlockSpec(memory_space=pltpu.VMEM)
    half = jax.ShapeDtypeStruct((slots.shape[0] // 2, 256), jnp.float32)
    return pl.pallas_call(
        gram_body,
        out_shape=(half, half),
        in_specs=[vmem] * 4,
        out_specs=(vmem, vmem),
        scratch_shapes=[
            pltpu.VMEM((16, depth, 2 * count), jnp.float32),
            pltpu.VMEM((16, depth, 2 * count), jnp.float32),
            pltpu.VMEM((256, 8, count), jnp.float32),
            pltpu.VMEM((256, count), jnp.bfloat16),
            pltpu.VMEM((256, count), jnp.bfloat16),
        ],
        compiler_params=pltpu.CompilerParams(vmem_limit_bytes=24 * 1024 * 1024),
        name="gram_sums",
    )(by_point, table, row_weights, slots)


def finish_body(parts_ref, unpack_ref, out_ref):
    total = jnp.sum(parts_ref[...], axis=0)
    first = total.astype(jnp.bfloat16)
    rest = total - first.astype(jnp.float32)
    second = rest.astype(jnp.bfloat16)
    third = (rest - second.astype(jnp.float32)).astype(jnp.bfloat16)
    rows = jnp.concatenate([first, second, third], axis=0)
    full = jnp.dot(rows, unpack_ref[...], preferred_element_type=jnp.float32)
    slots = total.shape[0]
    out_ref[...] = full[:slots] + full[slots : 2 * slots] + full[2 * slots :]


def finish(parts, unpack):
    vmem = pl.BlockSpec(memory_space=pltpu.VMEM)
    return pl.pallas_call(
        finish_body,
        out_shape=jax.ShapeDtypeStruct((parts.shape[1], unpack.shape[1]), jnp.float32),
        in_specs=[vmem] * 2,
        out_specs=vmem,
        compiler_params=pltpu.CompilerParams(vmem_limit_bytes=8 * 1024 * 1024),
        name="finish",
    )(parts, unpack)


def unpack_matrix(blocks):
    table = np.zeros((256, 2 * blocks * blocks), np.float32)
    half = blocks // 2
    for b in range(blocks):
        for e in range(blocks):
            delta = (e - b) % blocks
            if delta < half:
                real, imag, sign = 16 * delta + b, 16 * (delta + 7) + b, 1.0
            elif delta == half:
                real, imag, sign = 240 + b % half, 248 + b % half, 1.0 if b < half else -1.0
            else:
                back = blocks - delta
                real, imag, sign = 16 * back + e, 16 * (back + 7) + e, -1.0
            table[real, b * blocks + e] = 1.0
            if delta:
                table[imag, blocks * blocks + b * blocks + e] = sign
    return table


def shards(snapshots, weights, freq_bins, bin_owners):
    blocks, local_steps, fields, points = snapshots.shape
    tm_count = lax.axis_size("tm")
    pts_count = lax.axis_size("pts")
    fft_len = local_steps * tm_count
    sub_points = points // tm_count
    sent = scatter_points(jnp.transpose(snapshots, (0, 2, 1, 3)))
    by_point = exchange(sent, "tm", FIRST_POINTS)
    table = dft_columns(freq_bins, fft_len, FIRST_POINTS * local_steps)
    slots = slot_rows(bin_owners, tm_count, lax.axis_index("pts") & 1)
    mine = lax.dynamic_slice(weights, (0, lax.axis_index("tm") * sub_points), (fields, sub_points))
    row_weights = jnp.broadcast_to(mine[:, :, None], (fields, sub_points, LANES))
    row_weights = row_weights.reshape(fields * sub_points, LANES)
    keep, send = gram_sums(by_point, table, row_weights, slots)
    pairs = [(i, i ^ 1) for i in range(pts_count)]
    partial = (keep + lax.ppermute(send, "pts", pairs)).reshape(tm_count, CAP // 2, 256)
    partial = exchange(partial, "tm", FIRST_SLOTS)
    owned = jnp.sum(partial, axis=0)
    copies = jnp.broadcast_to(owned[None], (pts_count,) + owned.shape)
    copies = exchange(copies, "pts", FIRST_SUMS)
    parts = copies.reshape(pts_count // 2, CAP, 256)
    return finish(parts, jnp.asarray(unpack_matrix(blocks), jnp.bfloat16))


def solution(mesh):
    in_specs = (P(None, "tm", None, "pts"), P(None, "pts"), P(), P())
    out_specs = P("tm", None)
    return jax.shard_map(shards, mesh=mesh, in_specs=in_specs, out_specs=out_specs, check_vma=False)
```
